256 devices in a mesh: row: 16 (over y, x), col: 16 (over z, core).
Axes of the slice: x: 4, y: 4, z: 8, core: 2. Of those that a mesh axis runs over, the one named last changes fastest.
Arguments:
- factor_diag: float32 [2, 512, 512], replicated, as said below
- factor_mid: float32 [512, 512], replicated, may hold values from -0.25 to 0.25
- factor_low: float32 [2, 16384, 512], P(None, ('row', 'col')), may hold values from -0.046875 to 0.046875
- adjoint_diag: float32 [2, 512, 512], replicated, may hold values from -6 to 6
- adjoint_mid: float32 [512, 512], replicated, may hold values from -6 to 6
- adjoint_low: float32 [2, 16384, 512], P(None, ('row', 'col')), may hold values from -6 to 6
- trailing_adjoint: float32 [16384, 16, 1024], P('row', None, 'col'), as said below
Outputs:
- grad_diag: float32 [2, 512, 512], replicated
- grad_mid: float32 [512, 512], replicated
- grad_low: float32 [2, 16384, 512], P(None, ('row', 'col'))
The draws below stay inside these ranges and needn't reach their ends.
Inputs may be any that keep to these rules, and one draw needn't show every extreme that they name: `factor_diag`: each of the two [512, 512] blocks is lower triangular with diagonal entries between 1 and 2. `trailing_adjoint`: symmetric when read as an 16384 x 16384 matrix in row-major order.
All inputs are finite; a program needn't handle non-finite values.
Results may differ from the reference program's by a relative error of at most 0.000065.
Values sent between devices are 32-bit elements; how exact they have to be, the bound alone decides.
No kernel may reach another device: no remote copies, remote signals or barrier semaphores. Data moves between devices by JAX's collectives and lax.ppermute only.
A program may use at most 128 MiB of HBM per device.

```python
import math
import jax
import jax.numpy as jnp
from jax import lax

B = 512
R = 16384
N_ROW = 16


def draw_factor_diag(key, part):
    first_key, second_key = jax.random.split(jax.random.fold_in(key, 11))
    below = jax.random.normal(first_key, (2, B, B), jnp.float32) * (0.5 / math.sqrt(B))
    main_diag = jax.random.uniform(second_key, (2, B), jnp.float32, 1.0, 2.0)
    identity = jnp.eye(B, dtype=jnp.float32)
    return jnp.tril(below, -1) + main_diag[:, :, None] * identity[None, :, :]


def draw_trailing_adjoint(key, part):
    first_key = jax.random.fold_in(jax.random.fold_in(key, 23), 0)
    base = jax.random.normal(first_key, (R, R), jnp.float32)
    symmetric = (base + base.T) * 0.7071067811865476
    return symmetric.reshape(R, N_ROW, R // N_ROW)


def block_levels(own_key, extent, cuts, low, high):
    gain, own = 1.0, jax.random.fold_in(own_key, 6)
    for dim, parts in cuts:
        steps = jnp.exp(jax.random.uniform(jax.random.fold_in(own, dim), (parts,), jnp.float32, low / len(cuts), high / len(cuts)))
        gain = gain * jnp.repeat(steps, extent[dim] // parts).reshape([-1 if axis == dim else 1 for axis in range(len(extent))])
    return gain


def noise(stream_key, extent, spread, limit, cuts=(), kind=jnp.bfloat16):
    values = spread * jax.random.normal(stream_key, extent, jnp.float32)
    if cuts:
        values = values * block_levels(stream_key, extent, cuts, -0.22, 0.18)
    return jnp.clip(values, -limit, limit).astype(kind)


def setup_inputs(seed: int = 0) -> dict:
    streams_of = jax.random.split(jax.random.key(seed), 8)
    return {
        "factor_diag": draw_factor_diag(jax.random.fold_in(streams_of[7], 71), 0),
        "factor_mid": noise(streams_of[1], (B, B), B ** -0.5, 0.25, (), jnp.float32),
        "factor_low": noise(streams_of[2], (2, R, B), R ** -0.5, 0.046875, ((1, 256),), jnp.float32),
        "adjoint_diag": noise(streams_of[3], (2, B, B), 1.0, 6.0, (), jnp.float32),
        "adjoint_mid": noise(streams_of[4], (B, B), 1.0, 6.0, (), jnp.float32),
        "adjoint_low": noise(streams_of[5], (2, R, B), 1.0, 6.0, ((1, 256),), jnp.float32),
        "trailing_adjoint": draw_trailing_adjoint(jax.random.fold_in(streams_of[7], 71), 0),
    }


def lower_half(matrix):
    return jnp.tril(matrix, -1) + 0.5 * jnp.diag(jnp.diag(matrix))

def product(left_side, right_side):
    return jnp.dot(left_side.astype(jnp.float32), right_side.astype(jnp.float32), precision=lax.Precision.HIGHEST, preferred_element_type=jnp.float32)

def right_solve(factor, row_block):
    return jax.scipy.linalg.solve_triangular(factor, row_block.T, trans=1, lower=True).T

def diag_adjoint(factor, adjoint):
    inner_term = lower_half(product(factor.T, adjoint))
    halfway = jax.scipy.linalg.solve_triangular(factor, inner_term, trans=1, lower=True)
    whole_term = right_solve(factor, halfway)
    return 0.5 * (whole_term + whole_term.T)

def reference(factor_diag, factor_mid, factor_low, adjoint_diag, adjoint_mid, adjoint_low, trailing_adjoint):
    trailing = trailing_adjoint.reshape(R, R)
    second_solved = right_solve(factor_diag[1], adjoint_low[1] - 2.0 * product(trailing, factor_low[1]))
    second_adjoint = adjoint_diag[1] - product(second_solved.T, factor_low[1])
    second_grad = diag_adjoint(factor_diag[1], second_adjoint)
    second_half = 0.5 * second_solved
    top_rows = adjoint_mid - 2.0 * (product(second_grad, factor_mid) + product(second_half.T, factor_low[0]))
    top_solved = right_solve(factor_diag[0], top_rows)
    bottom_rows = adjoint_low[0] - 2.0 * (product(second_half, factor_mid) + product(trailing, factor_low[0]))
    bottom_solved = right_solve(factor_diag[0], bottom_rows)
    first_adjoint = adjoint_diag[0] - product(top_solved.T, factor_mid) - product(bottom_solved.T, factor_low[0])
    first_grad = diag_adjoint(factor_diag[0], first_adjoint)
    return (jnp.stack([first_grad, second_grad]), 0.5 * top_solved, jnp.stack([0.5 * bottom_solved, second_half]))
```

```python
import functools
import jax
import jax.numpy as jnp
from jax import lax
from jax.experimental import pallas as pl
from jax.experimental.pallas import tpu as pltpu
from jax.sharding import Mesh, PartitionSpec as P

SIZES = {"y": 4, "x": 4, "z": 8, "c": 2}
TILE = 128


F32 = jnp.float32
BF16 = jnp.bfloat16
VMEM = pl.BlockSpec(memory_space=pltpu.VMEM)
SMEM = pl.BlockSpec(memory_space=pltpu.SMEM)
NN, TN = ((1,), (0,)), ((0,), (0,))


def product(left_side, right_side, dims=NN):
    return lax.dot_general(
        left_side, right_side, (dims, ((), ())), precision=lax.Precision.HIGHEST, preferred_element_type=F32
    )


def split(value):
    high = value.astype(BF16)
    return high, (value - high.astype(F32)).astype(BF16)


def pair_product(left_side, right_side, dims=NN):
    one = functools.partial(lax.dot_general, dimension_numbers=(dims, ((), ())), preferred_element_type=F32)
    return (
        one(left_side[0], right_side[0])
        + (one(left_side[0], right_side[1]) + one(left_side[1], right_side[0]))
    )


def call(kernel, outs, flops, grid=None, in_specs=None, out_specs=None, scratch=()):
    specs = {} if grid is None else {"grid": grid}
    return pl.pallas_call(
        kernel,
        out_shape=outs,
        in_specs=in_specs,
        out_specs=out_specs,
        scratch_shapes=scratch,
        cost_estimate=pl.CostEstimate(flops=flops, bytes_accessed=8 * 2**20, transcendentals=0),
        **specs,
    )


def array(*shape):
    return jax.ShapeDtypeStruct(shape, F32)


def matmul(left_side, right_side, dims=NN):
    if dims == TN:
        left_side = left_side.T
    return pair_product(split(left_side), split(right_side))


def invert_kernel(factor, out, blocks, parts):
    count, size = factor.shape[0], factor.shape[1]
    row = lax.broadcasted_iota(jnp.int32, (TILE, TILE), 0)
    column = lax.broadcasted_iota(jnp.int32, (TILE, TILE), 1)
    eye = row == column
    per = size // TILE
    for p in range(count):
        for b in range(per):
            at = slice(b * TILE, (b + 1) * TILE)
            block = factor[p, at, at]
            blocks[p * per + b] = block
            parts[p * per + b] = jnp.where(eye, 1.0 / jnp.where(eye, block, 1.0), 0.0)

    def level(step, carry):
        high, low = lax.shift_right_logical(row, step), lax.shift_right_logical(column, step)
        corner = (high == low + 1) & ((high & 1) == 1)
        slots = range(count * per)
        halves = [product(jnp.where(corner, blocks[s], 0.0), parts[s]) for s in slots]
        news = [parts[s] - product(parts[s], halves[s]) for s in slots]
        for s in slots:
            parts[s] = news[s]
        return carry

    lax.fori_loop(0, TILE.bit_length() - 1, level, 0)
    out[...] = jnp.zeros_like(out)
    for p in range(count):
        for b in range(per):
            at = slice(b * TILE, (b + 1) * TILE)
            out[p, at, at] = parts[p * per + b]
    step = TILE
    while step < size:
        for p in range(count):
            for start in range(0, size, 2 * step):
                low, mid, high = start, start + step, start + 2 * step
                half = product(factor[p, mid:high, low:mid], out[p, low:mid, low:mid])
                out[p, mid:high, low:mid] = -product(out[p, mid:high, mid:high], half)
        step *= 2


def invert(factor_diag):
    count, size = factor_diag.shape[0], factor_diag.shape[1]
    blocks = pltpu.VMEM((count * size // TILE, TILE, TILE), F32)
    return call(
        invert_kernel, array(*factor_diag.shape), 10**10,
        in_specs=[VMEM], out_specs=VMEM, scratch=[blocks, blocks],
    )(factor_diag)


def constants_kernel(factor, mid, adjoint, adjoint_mid, inverses, solved, second, first):
    solved[...] = matmul(inverses[1], mid[...])
    second[...] = matmul(factor[1], adjoint[1], TN)
    first[...] = matmul(factor[0], adjoint[0], TN) - matmul(adjoint_mid[...], mid[...], TN)


def constants(factor_diag, factor_mid, adjoint_diag, adjoint_mid, inverses):
    square = array(*factor_mid.shape)
    return call(
        constants_kernel, (square, square, square), 5 * 10**9,
        in_specs=[VMEM] * 5, out_specs=(VMEM,) * 3,
    )(factor_diag, factor_mid, adjoint_diag, adjoint_mid, inverses)


def turn_kernel(block, high, low):
    high[...], low[...] = split(block[...].T)


def turn(flipped):
    count, depth = flipped.shape
    step = min(256, depth)
    out = jax.ShapeDtypeStruct((depth, count), BF16)
    tall = pl.BlockSpec((step, count), lambda i: (i, 0))
    return call(
        turn_kernel, (out, out), 10**9,
        grid=(depth // step,),
        in_specs=[pl.BlockSpec((count, step), lambda i: (0, i))],
        out_specs=(tall, tall),
    )(flipped)


def first_image_kernel(offsets, place, block, near, near_other, far, far_other, out, high, low):
    chip, core = place[0], place[1]
    rows = near.shape[1]

    @pl.when(pl.program_id(0) == 0)
    def _():
        index = 0
        for mine, other in ((near, near_other), (far, far_other)):
            for slot in range(mine.shape[0]):
                at = lax.rem(chip + offsets[index] + SIZES["z"], SIZES["z"]) * 2
                for ref, owner in ((mine, core), (other, 1 - core)):
                    where = pl.ds(pl.multiple_of((at + owner) * rows, rows), rows)
                    high[where, :], low[where, :] = split(ref[slot])
                index += 1

    out[...] = pair_product(split(block[...]), (high[...], low[...]))


def first_image(offsets, place, flipped, near, near_other, far, far_other):
    count, depth = flipped.shape
    size = near.shape[2]
    step = min(512, count)
    whole = lambda v: pl.BlockSpec(v.shape, lambda i: (0, 0, 0), pipeline_mode=pl.Buffered(1))
    gathered = (near, near_other, far, far_other)
    return call(
        functools.partial(first_image_kernel, offsets), array(count, size), 3 * 10**9,
        grid=(count // step,),
        in_specs=[SMEM, pl.BlockSpec((step, depth), lambda i: (i, 0))] + [whole(v) for v in gathered],
        out_specs=pl.BlockSpec((step, size), lambda i: (i, 0)),
        scratch=[pltpu.VMEM((depth, size), BF16)] * 2,
    )(place, flipped, *gathered)


def second_image_kernel(place, high, low, columns, keep, give, right_high, right_low):
    chip, core = place[0], place[1]
    rows = keep.shape[1]

    @pl.when(pl.program_id(0) == 0)
    def _():
        right_high[...], right_low[...] = split(columns[...])

    value = pair_product((high[...], low[...]), (right_high[...], right_low[...]))
    chips = value.shape[0] // (2 * rows)
    for n in range(chips):
        slot = lax.rem(pl.program_id(0) * chips + n - chip + SIZES["z"], SIZES["z"])
        even = value[2 * n * rows : (2 * n + 1) * rows, :]
        odd = value[(2 * n + 1) * rows : (2 * n + 2) * rows, :]
        keep[slot] = jnp.where(core == 0, even, odd)
        give[slot] = jnp.where(core == 0, odd, even)


def second_image(place, high, low, columns):
    depth, count = high.shape
    size = columns.shape[1]
    step = min(512, depth)
    tall = pl.BlockSpec((step, count), lambda i: (i, 0))
    rows = depth // (2 * SIZES["z"])
    out = array(SIZES["z"], rows, size)
    spec = pl.BlockSpec(out.shape, lambda i: (0, 0, 0))
    return call(
        second_image_kernel, (out, out), 3 * 10**9,
        grid=(depth // step,),
        in_specs=[
            SMEM, tall, tall, pl.BlockSpec((count, size), lambda i: (0, 0), pipeline_mode=pl.Buffered(1)),
        ],
        out_specs=(spec, spec),
        scratch=[pltpu.VMEM((count, size), BF16)] * 2,
    )(place, high, low, columns)


def terms_kernel(place, second_sum, pieces, adjoint, factor, keep, give, rows, second_second, second_first, first_first):
    size = second_sum.shape[1]
    per = size // TILE
    middle = size // 2
    first_sum = pieces[0]
    for n in range(1, pieces.shape[0]):
        first_sum = first_sum + pieces[n]
    second = adjoint[1] - 2.0 * second_sum[...]
    first = adjoint[0] - 2.0 * first_sum
    rows[1], rows[0] = second, first

    def put(ref, at, cols, left, right):
        ref[at, cols] = pair_product(tuple(v[at, :] for v in left), tuple(v[:, cols] for v in right))

    second, first = split(second.T), split(first.T)
    second_right, first_right = split(factor[1]), split(factor[0])
    top, low, full = slice(0, middle), slice(middle, size), slice(0, size)
    put(second_first, full, full, second, first_right)
    put(second_second, top, top, second, second_right)
    put(second_second, low, full, second, second_right)
    put(first_first, top, top, first, first_right)
    put(first_first, low, full, first, first_right)

    lower = [(i, j) for i in range(per) for j in range(i + 1)]
    square = [(i, j) for i in range(per) for j in range(per)]
    tiles = [(second_second, at) for at in lower] + [(second_first, at) for at in square]
    tiles += [(first_first, at) for at in lower]
    half = len(tiles) // 2

    def store(out, chosen):
        for n, (ref, (i, j)) in enumerate(chosen):
            out[n * TILE : (n + 1) * TILE, :] = ref[
                i * TILE : (i + 1) * TILE, j * TILE : (j + 1) * TILE
            ]

    @pl.when(place[1] == 0)
    def _():
        store(keep, tiles[:half])
        store(give, tiles[half:])

    @pl.when(place[1] == 1)
    def _():
        store(keep, tiles[half:])
        store(give, tiles[:half])


def terms(place, second_sum, pieces, adjoint_low, factor_low):
    size = second_sum.shape[1]
    per = size // TILE
    half = per * (2 * per + 1) // 2 * TILE
    return call(
        terms_kernel, (array(half, TILE), array(half, TILE), array(*adjoint_low.shape)), 10**9,
        in_specs=[SMEM] + [VMEM] * 4,
        out_specs=(VMEM,) * 3,
        scratch=[pltpu.VMEM((size, size), F32)] * 3,
    )(place, second_sum, pieces, adjoint_low, factor_low)


def rows_kernel(rows, inverses, solved, out):
    out[1] = 0.5 * matmul(rows[1], inverses[1])
    out[0] = 0.5 * matmul(rows[0] - matmul(rows[1], solved[...]), inverses[0])


def finish_kernel(
    place, mine, other, inverses, solved, second_const, first_const, adjoint_mid, diag, top, second, cross, first
):
    size = solved.shape[0]
    core = place[1]
    per = size // TILE
    half = mine.shape[0] // TILE
    upper = lax.broadcasted_iota(jnp.int32, (TILE, TILE), 0) < lax.broadcasted_iota(
        jnp.int32, (TILE, TILE), 1
    )

    def tile(index):
        part, row = divmod(index, half)
        rows = slice(row * TILE, (row + 1) * TILE)
        return jnp.where(core == part, mine[rows, :], other[rows, :])

    def at(i, j):
        return (slice(i * TILE, (i + 1) * TILE), slice(j * TILE, (j + 1) * TILE))

    def mirror(value, ref):
        for i in range(per):
            for j in range(i + 1):
                part = value(i, j)
                if i == j:
                    ref[at(i, j)] = jnp.where(upper, part.T, part)
                else:
                    ref[at(i, j)] = part
                    ref[at(j, i)] = part.T

    low = per * (per + 1) // 2
    number = lambda i, j: i * (i + 1) // 2 + j
    mirror(lambda i, j: second_const[at(i, j)] - tile(number(i, j)), second)
    for i in range(per):
        for j in range(per):
            cross[at(i, j)] = tile(low + i * per + j)
    known = solved[...]
    image = matmul(second[...], known)
    outer = matmul(known, 0.5 * image + cross[...], TN)
    outer = outer + outer.T

    def first_value(i, j):
        return first_const[at(i, j)] - tile(low + per * per + number(i, j)) + outer[at(i, j)]

    mirror(first_value, first)
    diag[0] = 0.5 * matmul(matmul(inverses[0], first[...], TN), inverses[0])
    diag[1] = 0.5 * matmul(matmul(inverses[1], second[...], TN), inverses[1])
    rest = adjoint_mid[...] - matmul(inverses[1], image + cross[...], TN)
    top[...] = 0.5 * matmul(rest, inverses[0])


def finish(place, tiles, other, inverses, mid_solved, second_const, first_const, adjoint_mid):
    size = mid_solved.shape[0]
    return call(
        finish_kernel, (array(2, size, size), array(size, size)), 10**10,
        in_specs=[SMEM] + [VMEM] * 7, out_specs=(VMEM, VMEM),
        scratch=[pltpu.VMEM((size, size), F32)] * 3,
    )(place, tiles, other, inverses, mid_solved, second_const, first_const, adjoint_mid)


def shift(value, axis, step):
    size = SIZES[axis]
    return lax.ppermute(value, axis, [(i, (i + step) % size) for i in range(size)])


def ring_sum(blocks, axis):
    size = SIZES[axis]
    far = blocks[size // 2]
    half = far.shape[0] // 2
    ahead, behind = shift(far[:half], axis, 1), shift(far[half:], axis, -1)
    for step in range(size // 2 - 1, 0, -1):
        up, down = blocks[step], blocks[size - step]
        if step == size // 2 - 1:
            up = jnp.concatenate([up[:half] + ahead, up[half:]])
            down = jnp.concatenate([down[:half], down[half:] + behind])
        else:
            up, down = up + ahead, down + behind
        ahead, behind = shift(up, axis, 1), shift(down, axis, -1)
    return blocks[0] + ahead + behind


def spread(value, axes, parts):
    return lax.all_to_all(jnp.broadcast_to(value[None], (parts,) + value.shape), axes, 0, 0)


def shards(
    factor_diag, factor_mid, factor_low, adjoint_diag, adjoint_mid, adjoint_low, trailing_adjoint
):
    size = factor_mid.shape[0]
    rows = factor_low.shape[1]
    block_rows, row_groups, group_cols = trailing_adjoint.shape
    flipped = trailing_adjoint.transpose(1, 2, 0).reshape(row_groups * group_cols, block_rows)
    place = jnp.stack([lax.axis_index("z"), lax.axis_index("c")]).astype(jnp.int32)
    parts = SIZES["y"] * SIZES["x"]

    columns = spread(factor_low[1], ("y", "x"), parts).reshape(-1, size)

    own, half = factor_low[0], rows // 2
    ahead, behind = [own], [own]
    for _ in range(1, 4):
        ahead.append(shift(ahead[-1], "z", 1))
        behind.append(shift(behind[-1], "z", -1))
    across = jnp.concatenate([shift(ahead[3][:half], "z", 1), shift(behind[3][half:], "z", -1)])
    near = jnp.stack([own, ahead[1], behind[1], ahead[2], behind[2]])
    far = jnp.stack([ahead[3], behind[3], across])
    high, low = turn(flipped)
    images = first_image(
        (0, -1, 1, -2, 2, -3, 3, 4), place, flipped, near, shift(near, "c", 1), far, shift(far, "c", 1)
    )
    pieces = lax.all_to_all(images.reshape(parts, rows, size), ("y", "x"), 0, 0)
    keep, give = second_image(place, high, low, columns)
    second_sum = ring_sum(keep + shift(give, "c", 1), "z")

    keep, give, sides = terms(place, second_sum, pieces, adjoint_low, factor_low)
    keep = keep + shift(give, "c", 1)
    tiles = lax.all_to_all(keep.reshape(parts, -1, TILE), ("y", "x"), 0, 0)
    tiles = spread(tiles.sum(0), "z", SIZES["z"])
    tiles = spread(tiles.sum(0), ("y", "x"), parts).reshape(-1, TILE)
    other = shift(tiles, "c", 1)
    inverses = invert(factor_diag)
    mid_solved, second_const, first_const = constants(
        factor_diag, factor_mid, adjoint_diag, adjoint_mid, inverses
    )
    low = call(
        rows_kernel, array(2, rows, size), 10**9, in_specs=[VMEM] * 3, out_specs=VMEM
    )(sides, inverses, mid_solved)
    diag, top = finish(place, tiles, other, inverses, mid_solved, second_const, first_const, adjoint_mid)
    return diag, top, low


def solution(mesh):
    axes = tuple(SIZES)
    torus = Mesh(mesh.devices.reshape(tuple(SIZES.values())), axes)
    low = P(None, axes, None)

    return jax.shard_map(
        shards,
        mesh=torus,
        in_specs=(P(), P(), low, P(), P(), low, P(("y", "x"), None, ("z", "c"))),
        out_specs=(P(), P(), low),
        check_vma=False,
    )
```

```python
import functools
import jax
import jax.numpy as jnp
from jax import lax
from jax.experimental import pallas as pl
from jax.experimental.pallas import tpu as pltpu
from jax.sharding import Mesh, PartitionSpec as P

SIZES = {"y": 4, "x": 4, "z": 8, "c": 2}
TILE = 128


F32 = jnp.float32
BF16 = jnp.bfloat16
VMEM = pl.BlockSpec(memory_space=pltpu.VMEM)
SMEM = pl.BlockSpec(memory_space=pltpu.SMEM)
NN, TN = ((1,), (0,)), ((0,), (0,))


def product(left_side, right_side, dims=NN):
    return lax.dot_general(
        left_side, right_side, (dims, ((), ())), precision=lax.Precision.HIGHEST, preferred_element_type=F32
    )


def split(value):
    high = value.astype(BF16)
    return high, (value - high.astype(F32)).astype(BF16)


def pair_product(left_side, right_side, dims=NN):
    one = functools.partial(lax.dot_general, dimension_numbers=(dims, ((), ())), preferred_element_type=F32)
    return (
        one(left_side[0], right_side[0])
        + (one(left_side[0], right_side[1]) + one(left_side[1], right_side[0]))
    )


def call(kernel, outs, flops, grid=None, in_specs=None, out_specs=None, scratch=(), limit=None):
    specs = {} if grid is None else {"grid": grid}
    return pl.pallas_call(
        kernel,
        out_shape=outs,
        in_specs=in_specs,
        out_specs=out_specs,
        scratch_shapes=scratch,
        compiler_params=pltpu.CompilerParams(vmem_limit_bytes=limit),
        cost_estimate=pl.CostEstimate(flops=flops, bytes_accessed=8 * 2**20, transcendentals=0),
        **specs,
    )


def array(*shape):
    return jax.ShapeDtypeStruct(shape, F32)


def near_core(*values):
    return tuple(pltpu.with_memory_space_constraint(v, pltpu.VMEM) for v in values)


def far_core(*values):
    return tuple(pltpu.with_memory_space_constraint(v, pltpu.HBM) for v in values)


def matmul(left_side, right_side, dims=NN):
    if dims == TN:
        left_side = left_side.T
    return pair_product(split(left_side), split(right_side))


def invert_kernel(factor, out, blocks, parts):
    count, size = factor.shape[0], factor.shape[1]
    row = lax.broadcasted_iota(jnp.int32, (TILE, TILE), 0)
    column = lax.broadcasted_iota(jnp.int32, (TILE, TILE), 1)
    eye = row == column
    per = size // TILE
    for p in range(count):
        for b in range(per):
            at = slice(b * TILE, (b + 1) * TILE)
            block = factor[p, at, at]
            blocks[p * per + b] = block
            parts[p * per + b] = jnp.where(eye, 1.0 / jnp.where(eye, block, 1.0), 0.0)

    def level(step, carry):
        high, low = lax.shift_right_logical(row, step), lax.shift_right_logical(column, step)
        corner = (high == low + 1) & ((high & 1) == 1)
        slots = range(count * per)
        halves = [product(jnp.where(corner, blocks[s], 0.0), parts[s]) for s in slots]
        news = [parts[s] - product(parts[s], halves[s]) for s in slots]
        for s in slots:
            parts[s] = news[s]
        return carry

    lax.fori_loop(0, TILE.bit_length() - 1, level, 0)
    out[...] = jnp.zeros_like(out)
    for p in range(count):
        for b in range(per):
            at = slice(b * TILE, (b + 1) * TILE)
            out[p, at, at] = parts[p * per + b]
    step = TILE
    while step < size:
        for p in range(count):
            for start in range(0, size, 2 * step):
                low, mid, high = start, start + step, start + 2 * step
                half = product(factor[p, mid:high, low:mid], out[p, low:mid, low:mid])
                out[p, mid:high, low:mid] = -product(out[p, mid:high, mid:high], half)
        step *= 2


def invert(factor_diag):
    count, size = factor_diag.shape[0], factor_diag.shape[1]
    blocks = pltpu.VMEM((count * size // TILE, TILE, TILE), F32)
    return call(
        invert_kernel, array(*factor_diag.shape), 10**10,
        in_specs=[VMEM], out_specs=VMEM, scratch=[blocks, blocks],
    )(*far_core(factor_diag))


def constants_kernel(factor, mid, adjoint, adjoint_mid, inverses, solved, second, first):
    solved[...] = matmul(inverses[1], mid[...])
    second[...] = matmul(factor[1], adjoint[1], TN)
    first[...] = matmul(factor[0], adjoint[0], TN) - matmul(adjoint_mid[...], mid[...], TN)


def constants(factor_diag, factor_mid, adjoint_diag, adjoint_mid, inverses):
    square = array(*factor_mid.shape)
    return call(
        constants_kernel, (square, square, square), 5 * 10**9,
        in_specs=[VMEM] * 5, out_specs=(VMEM,) * 3,
    )(*far_core(factor_diag, factor_mid, adjoint_diag, adjoint_mid, inverses))


def turn_kernel(block, high, low):
    high[...], low[...] = split(block[...].T)


def turn(flipped, part):
    count, depth = flipped.shape
    step = min(256, depth // 2)
    steps = depth // 2 // step
    out = jax.ShapeDtypeStruct((depth // 2, count), BF16)
    tall = pl.BlockSpec((step, count), lambda i: (i, 0))
    return call(
        turn_kernel, (out, out), 10**9,
        grid=(steps,),
        in_specs=[pl.BlockSpec((count, step), lambda i: (0, part * steps + i))],
        out_specs=(tall, tall),
    )(*far_core(flipped))


def first_image_kernel(offsets, place, block, near, near_other, far, far_other, out, high, low):
    chip, core = place[0], place[1]
    rows = near.shape[1]

    @pl.when(pl.program_id(0) == 0)
    def _():
        index = 0
        for mine, other in ((near, near_other), (far, far_other)):
            for slot in range(mine.shape[0]):
                at = lax.rem(chip + offsets[index] + SIZES["z"], SIZES["z"]) * 2
                for ref, owner in ((mine, core), (other, 1 - core)):
                    where = pl.ds(pl.multiple_of((at + owner) * rows, rows), rows)
                    high[where, :], low[where, :] = split(ref[slot])
                index += 1

    out[...] = pair_product(split(block[...]), (high[...], low[...]))


def first_image(offsets, place, flipped, near, near_other, far, far_other):
    count, depth = flipped.shape
    size = near.shape[2]
    step = min(512, count)
    gathered = near_core(near, near_other, far, far_other)
    return call(
        functools.partial(first_image_kernel, offsets), array(count, size), 3 * 10**9, limit=32 * 2**20,
        grid=(count // step,),
        in_specs=[SMEM, pl.BlockSpec((step, depth), lambda i: (i, 0))] + [VMEM] * 4,
        out_specs=pl.BlockSpec((step, size), lambda i: (i, 0)),
        scratch=[pltpu.VMEM((depth, size), BF16)] * 2,
    )(place, *far_core(flipped), *gathered)


def second_image_kernel(place, *refs):
    turned, (columns, keep, give) = refs[:-3], refs[-3:]
    chip, core = place[0], place[1]
    rows = keep.shape[1]
    right = split(columns[...])
    for part in range(len(turned) // 2):
        value = pair_product((turned[2 * part][...], turned[2 * part + 1][...]), right)
        chips = value.shape[0] // (2 * rows)
        for n in range(chips):
            slot = lax.rem(part * chips + n - chip + SIZES["z"], SIZES["z"])
            even = value[2 * n * rows : (2 * n + 1) * rows, :]
            odd = value[(2 * n + 1) * rows : (2 * n + 2) * rows, :]
            keep[slot] = jnp.where(core == 0, even, odd)
            give[slot] = jnp.where(core == 0, odd, even)


def second_image(place, turned, columns):
    depth, size = 2 * turned[0].shape[0], columns.shape[1]
    out = array(SIZES["z"], depth // (2 * SIZES["z"]), size)
    return call(
        second_image_kernel, (out, out), 3 * 10**9, limit=32 * 2**20,
        in_specs=[SMEM] + [VMEM] * (len(turned) + 1),
        out_specs=(VMEM, VMEM),
    )(place, *far_core(*turned), *near_core(columns))


def terms_kernel(place, second_sum, pieces, adjoint, factor, keep, give, rows, second_second, second_first, first_first):
    size = second_sum.shape[1]
    per = size // TILE
    middle = size // 2
    first_sum = pieces[0]
    for n in range(1, pieces.shape[0]):
        first_sum = first_sum + pieces[n]
    second = adjoint[1] - 2.0 * second_sum[...]
    first = adjoint[0] - 2.0 * first_sum
    rows[1], rows[0] = second, first

    def put(ref, at, cols, left, right):
        ref[at, cols] = pair_product(tuple(v[at, :] for v in left), tuple(v[:, cols] for v in right))

    second, first = split(second.T), split(first.T)
    second_right, first_right = split(factor[1]), split(factor[0])
    top, low, full = slice(0, middle), slice(middle, size), slice(0, size)
    put(second_first, full, full, second, first_right)
    put(second_second, top, top, second, second_right)
    put(second_second, low, full, second, second_right)
    put(first_first, top, top, first, first_right)
    put(first_first, low, full, first, first_right)

    lower = [(i, j) for i in range(per) for j in range(i + 1)]
    square = [(i, j) for i in range(per) for j in range(per)]
    tiles = [(second_second, at) for at in lower] + [(second_first, at) for at in square]
    tiles += [(first_first, at) for at in lower]
    half = len(tiles) // 2

    def store(out, chosen):
        for n, (ref, (i, j)) in enumerate(chosen):
            out[n * TILE : (n + 1) * TILE, :] = ref[
                i * TILE : (i + 1) * TILE, j * TILE : (j + 1) * TILE
            ]

    @pl.when(place[1] == 0)
    def _():
        store(keep, tiles[:half])
        store(give, tiles[half:])

    @pl.when(place[1] == 1)
    def _():
        store(keep, tiles[half:])
        store(give, tiles[:half])


def terms(place, second_sum, pieces, adjoint_low, factor_low):
    size = second_sum.shape[1]
    per = size // TILE
    half = per * (2 * per + 1) // 2 * TILE
    return call(
        terms_kernel, (array(half, TILE), array(half, TILE), array(*adjoint_low.shape)), 10**9, limit=32 * 2**20,
        in_specs=[SMEM] + [VMEM] * 4,
        out_specs=(VMEM,) * 3,
        scratch=[pltpu.VMEM((size, size), F32)] * 3,
    )(place, *near_core(second_sum, pieces), *far_core(adjoint_low, factor_low))


def rows_kernel(rows, inverses, solved, out):
    out[1] = 0.5 * matmul(rows[1], inverses[1])
    out[0] = 0.5 * matmul(rows[0] - matmul(rows[1], solved[...]), inverses[0])


def finish_kernel(
    place, mine, other, inverses, solved, second_const, first_const, adjoint_mid, diag, top, second, cross, first
):
    size = solved.shape[0]
    core = place[1]
    per = size // TILE
    half = mine.shape[0] // TILE
    upper = lax.broadcasted_iota(jnp.int32, (TILE, TILE), 0) < lax.broadcasted_iota(
        jnp.int32, (TILE, TILE), 1
    )

    def tile(index):
        part, row = divmod(index, half)
        rows = slice(row * TILE, (row + 1) * TILE)
        return jnp.where(core == part, mine[rows, :], other[rows, :])

    def at(i, j):
        return (slice(i * TILE, (i + 1) * TILE), slice(j * TILE, (j + 1) * TILE))

    def mirror(value, ref):
        for i in range(per):
            for j in range(i + 1):
                part = value(i, j)
                if i == j:
                    ref[at(i, j)] = jnp.where(upper, part.T, part)
                else:
                    ref[at(i, j)] = part
                    ref[at(j, i)] = part.T

    low = per * (per + 1) // 2
    number = lambda i, j: i * (i + 1) // 2 + j
    mirror(lambda i, j: second_const[at(i, j)] - tile(number(i, j)), second)
    for i in range(per):
        for j in range(per):
            cross[at(i, j)] = tile(low + i * per + j)
    middle = size // 2
    whole, top_half, low_half = slice(0, size), slice(0, middle), slice(middle, size)

    def part(pair, rows, cols):
        return tuple(v[rows, cols] for v in pair)

    def times_lower(left, lower):
        return jnp.concatenate(
            [
                pair_product(left, part(lower, whole, top_half)),
                pair_product(part(left, whole, low_half), part(lower, low_half, low_half)),
            ],
            axis=1,
        )

    def upper_times(upper, right):
        return jnp.concatenate(
            [
                pair_product(part(upper, top_half, whole), right),
                pair_product(part(upper, low_half, low_half), part(right, low_half, whole)),
            ]
        )

    def between(upper, symmetric, lower, out):
        half_way = split(times_lower(symmetric, lower))
        out[top_half, top_half] = 0.5 * pair_product(
            part(upper, top_half, whole), part(half_way, whole, top_half)
        )
        bottom = 0.5 * pair_product(
            part(upper, low_half, low_half), part(half_way, low_half, whole)
        )
        out[low_half, whole] = bottom
        out[top_half, low_half] = bottom[:, top_half].T

    first_lower, second_lower = split(inverses[0]), split(inverses[1])
    first_upper, second_upper = split(inverses[0].T), split(inverses[1].T)
    second_symmetric = split(second[...])
    image = pair_product(second_symmetric, split(solved[...]))
    outer = pair_product(split(solved[...].T), split(0.5 * image + cross[...]))
    outer = outer + outer.T

    def first_value(i, j):
        return first_const[at(i, j)] - tile(low + per * per + number(i, j)) + outer[at(i, j)]

    mirror(first_value, first)
    between(first_upper, split(first[...]), first_lower, diag.at[0])
    between(second_upper, second_symmetric, second_lower, diag.at[1])
    rest = adjoint_mid[...] - upper_times(second_upper, split(image + cross[...]))
    top[...] = 0.5 * times_lower(split(rest), first_lower)


def finish(place, tiles, other, inverses, mid_solved, second_const, first_const, adjoint_mid):
    size = mid_solved.shape[0]
    return call(
        finish_kernel, (array(2, size, size), array(size, size)), 10**10, limit=32 * 2**20,
        in_specs=[SMEM] + [VMEM] * 7, out_specs=(VMEM, VMEM),
        scratch=[pltpu.VMEM((size, size), F32)] * 3,
    )(
        place, *near_core(tiles, other),
        *far_core(inverses, mid_solved, second_const, first_const, adjoint_mid),
    )


def shift(value, axis, step):
    size = SIZES[axis]
    return lax.ppermute(value, axis, [(i, (i + step) % size) for i in range(size)])


def ring_sum(blocks, axis):
    size = SIZES[axis]
    far = blocks[size // 2]
    half = far.shape[0] // 2
    ahead = shift(far[:half], axis, 1)
    behind = shift(far[half:], axis, -1)
    for step in range(size // 2 - 1, 0, -1):
        up, down = blocks[step], blocks[size - step]
        if step == size // 2 - 1:
            up = jnp.concatenate([up[:half] + ahead, up[half:]])
            down = jnp.concatenate([down[:half], down[half:] + behind])
        else:
            up, down = up + ahead, down + behind
        ahead, behind = shift(up, axis, 1), shift(down, axis, -1)
    return blocks[0] + ahead + behind


def spread(value, axes, parts):
    return lax.all_to_all(jnp.broadcast_to(value[None], (parts,) + value.shape), axes, 0, 0)


def shards(
    factor_diag, factor_mid, factor_low, adjoint_diag, adjoint_mid, adjoint_low, trailing_adjoint
):
    size = factor_mid.shape[0]
    rows = factor_low.shape[1]
    block_rows, row_groups, group_cols = trailing_adjoint.shape
    flipped = trailing_adjoint.transpose(1, 2, 0).reshape(row_groups * group_cols, block_rows)
    place = jnp.stack([lax.axis_index("z"), lax.axis_index("c")]).astype(jnp.int32)
    parts = SIZES["y"] * SIZES["x"]

    columns = spread(factor_low[1], ("y", "x"), parts).reshape(-1, size)

    own, half = factor_low[0], rows // 2
    ahead, behind = [own], [own]
    for _ in range(1, 4):
        ahead.append(shift(ahead[-1], "z", 1))
        behind.append(shift(behind[-1], "z", -1))
    across = jnp.concatenate([shift(ahead[3][:half], "z", 1), shift(behind[3][half:], "z", -1)])
    near = jnp.stack([own, ahead[1], behind[1], ahead[2], behind[2]])
    far = jnp.stack([ahead[3], behind[3], across])
    near_other, far_other = shift(near, "c", 1), shift(far, "c", 1)
    turned = turn(flipped, 0)
    turned += turn(flipped, 1)
    images = first_image(
        (0, -1, 1, -2, 2, -3, 3, 4), place, flipped, near, near_other, far, far_other
    )
    pieces = lax.all_to_all(images.reshape(parts, rows, size), ("y", "x"), 0, 0)
    keep, give = second_image(place, turned, columns)
    give = shift(give, "c", 1)
    second_sum = ring_sum(keep + give, "z")

    keep, give, sides = terms(place, second_sum, pieces, adjoint_low, factor_low)
    keep = keep + shift(give, "c", 1)
    tiles = lax.all_to_all(keep.reshape(parts, -1, TILE), ("y", "x"), 0, 0)
    tiles = spread(tiles.sum(0), "z", SIZES["z"])
    tiles = spread(tiles.sum(0), ("y", "x"), parts).reshape(-1, TILE)
    other = shift(tiles, "c", 1)
    inverses = invert(factor_diag)
    mid_solved, second_const, first_const = constants(
        factor_diag, factor_mid, adjoint_diag, adjoint_mid, inverses
    )
    low = call(
        rows_kernel, array(2, rows, size), 10**9, in_specs=[VMEM] * 3, out_specs=VMEM
    )(*far_core(sides, inverses, mid_solved))
    diag, top = finish(place, tiles, other, inverses, mid_solved, second_const, first_const, adjoint_mid)
    return diag, top, low


def solution(mesh):
    axes = tuple(SIZES)
    torus = Mesh(mesh.devices.reshape(tuple(SIZES.values())), axes)
    low = P(None, axes, None)

    return jax.shard_map(
        shards,
        mesh=torus,
        in_specs=(P(), P(), low, P(), P(), low, P(("y", "x"), None, ("z", "c"))),
        out_specs=(P(), P(), low),
        check_vma=False,
    )
```

```python
import functools
import jax
import jax.numpy as jnp
from jax import lax
from jax.experimental import pallas as pl
from jax.experimental.pallas import tpu as pltpu
from jax.sharding import Mesh, PartitionSpec as P

SIZES = {"y": 4, "x": 4, "z": 8, "c": 2}
TILE = 128


F32 = jnp.float32
BF16 = jnp.bfloat16
VMEM = pl.BlockSpec(memory_space=pltpu.VMEM)
SMEM = pl.BlockSpec(memory_space=pltpu.SMEM)
APART = pl.BlockSpec(memory_space=pl.ANY)
NN, TN = ((1,), (0,)), ((0,), (0,))


def product(left_side, right_side, dims=NN):
    return lax.dot_general(
        left_side, right_side, (dims, ((), ())), precision=lax.Precision.HIGHEST, preferred_element_type=F32
    )


def split(value):
    high = value.astype(BF16)
    return high, (value - high.astype(F32)).astype(BF16)


def pair_product(left_side, right_side, dims=NN):
    one = functools.partial(lax.dot_general, dimension_numbers=(dims, ((), ())), preferred_element_type=F32)
    return (
        one(left_side[0], right_side[0])
        + (one(left_side[0], right_side[1]) + one(left_side[1], right_side[0]))
    )


def call(kernel, outs, flops, grid=None, in_specs=None, out_specs=None, scratch=(), limit=None):
    specs = {} if grid is None else {"grid": grid}
    return pl.pallas_call(
        kernel,
        out_shape=outs,
        in_specs=in_specs,
        out_specs=out_specs,
        scratch_shapes=scratch,
        compiler_params=pltpu.CompilerParams(vmem_limit_bytes=limit),
        cost_estimate=pl.CostEstimate(flops=flops, bytes_accessed=8 * 2**20, transcendentals=0),
        **specs,
    )


def array(*shape):
    return jax.ShapeDtypeStruct(shape, F32)


def near_core(*values):
    return tuple(pltpu.with_memory_space_constraint(v, pltpu.VMEM) for v in values)


def far_core(*values):
    return tuple(pltpu.with_memory_space_constraint(v, pltpu.HBM) for v in values)


def matmul(left_side, right_side, dims=NN):
    if dims == TN:
        left_side = left_side.T
    return pair_product(split(left_side), split(right_side))


def invert_kernel(factor, out, blocks, parts):
    count, size = factor.shape[0], factor.shape[1]
    row = lax.broadcasted_iota(jnp.int32, (TILE, TILE), 0)
    column = lax.broadcasted_iota(jnp.int32, (TILE, TILE), 1)
    eye = row == column
    per = size // TILE
    for p in range(count):
        for b in range(per):
            at = slice(b * TILE, (b + 1) * TILE)
            block = factor[p, at, at]
            blocks[p * per + b] = block
            parts[p * per + b] = jnp.where(eye, 1.0 / jnp.where(eye, block, 1.0), 0.0)

    def level(index, carry):
        step, group = lax.div(index, count), lax.rem(index, count) * per
        high, low = lax.shift_right_logical(row, step), lax.shift_right_logical(column, step)
        corner = (high == low + 1) & ((high & 1) == 1)
        slots = [group + b for b in range(per)]
        halves = [product(jnp.where(corner, blocks[s], 0.0), parts[s]) for s in slots]
        news = [parts[s] - product(parts[s], half) for s, half in zip(slots, halves)]
        for s, new in zip(slots, news):
            parts[s] = new
        return carry

    lax.fori_loop(0, (TILE.bit_length() - 1) * count, level, 0)
    out[...] = jnp.zeros_like(out)
    for p in range(count):
        for b in range(per):
            at = slice(b * TILE, (b + 1) * TILE)
            out[p, at, at] = parts[p * per + b]
    step = TILE
    while step < size:
        for p in range(count):
            for start in range(0, size, 2 * step):
                low, mid, high = start, start + step, start + 2 * step
                half = product(factor[p, mid:high, low:mid], out[p, low:mid, low:mid])
                out[p, mid:high, low:mid] = -product(out[p, mid:high, mid:high], half)
        step *= 2


def invert(factor_diag):
    count, size = factor_diag.shape[0], factor_diag.shape[1]
    blocks = pltpu.VMEM((count * size // TILE, TILE, TILE), F32)
    return call(
        invert_kernel, array(*factor_diag.shape), 10**10,
        in_specs=[VMEM], out_specs=VMEM, scratch=[blocks, blocks],
    )(*far_core(factor_diag))


def constants_kernel(factor, mid, adjoint, adjoint_mid, inverses, solved, second, first):
    solved[...] = matmul(inverses[1], mid[...])
    second[...] = matmul(factor[1], adjoint[1], TN)
    first[...] = matmul(factor[0], adjoint[0], TN) - matmul(adjoint_mid[...], mid[...], TN)


def constants(factor_diag, factor_mid, adjoint_diag, adjoint_mid, inverses):
    square = array(*factor_mid.shape)
    return call(
        constants_kernel, (square, square, square), 5 * 10**9,
        in_specs=[VMEM] * 5, out_specs=(VMEM,) * 3,
    )(*far_core(factor_diag, factor_mid, adjoint_diag, adjoint_mid, inverses))


def turn_kernel(block, high, low):
    high[...], low[...] = split(block[...].T)


def turn(flipped, part):
    count, depth = flipped.shape
    step = min(256, depth // 2)
    steps = depth // 2 // step
    out = jax.ShapeDtypeStruct((depth // 2, count), BF16)
    tall = pl.BlockSpec((step, count), lambda i: (i, 0))
    return call(
        turn_kernel, (out, out), 10**9,
        grid=(steps,),
        in_specs=[pl.BlockSpec((count, step), lambda i: (0, part * steps + i))],
        out_specs=(tall, tall),
    )(*far_core(flipped))


def first_image_kernel(place, block, near, near_other, far, far_other, out, high, low):
    chip, core = place[0], place[1]
    rows = near.shape[1]

    @pl.when(pl.program_id(0) == 0)
    def _():
        start = 0
        for mine, other in ((near, near_other), (far, far_other)):

            def put(slot, carry, start=start, mine=mine, other=other):
                index = start + slot
                distance = lax.div(index + 1, 2)
                offset = jnp.where(lax.rem(index, 2) == 1, -distance, distance)
                at = lax.rem(chip + offset + SIZES["z"], SIZES["z"]) * 2
                for ref, owner in ((mine, core), (other, 1 - core)):
                    where = pl.ds(pl.multiple_of((at + owner) * rows, rows), rows)
                    high[where, :], low[where, :] = split(ref[slot])
                return carry

            lax.fori_loop(0, mine.shape[0], put, 0)
            start += mine.shape[0]

    out[...] = pair_product(split(block[...]), (high[...], low[...]))


def first_image(place, flipped, near, near_other, far, far_other):
    count, depth = flipped.shape
    size = near.shape[2]
    step = min(512, count)
    gathered = near_core(near, near_other, far, far_other)
    return call(
        first_image_kernel, array(count, size), 3 * 10**9, limit=32 * 2**20,
        grid=(count // step,),
        in_specs=[SMEM, pl.BlockSpec((step, depth), lambda i: (i, 0))] + [VMEM] * 4,
        out_specs=pl.BlockSpec((step, size), lambda i: (i, 0)),
        scratch=[pltpu.VMEM((depth, size), BF16)] * 2,
    )(place, *far_core(flipped), *gathered)


def second_image_kernel(place, *refs):
    turned, (columns, keep, give, held, done) = refs[:-5], refs[-5:]
    chip, core = place[0], place[1]
    rows = keep.shape[1]
    copies = [pltpu.make_async_copy(v, held.at[n], done.at[n]) for n, v in enumerate(turned)]
    for copy in copies:
        copy.start()
    right = split(columns[...])
    for part in range(len(turned) // 2):
        copies[2 * part].wait()
        copies[2 * part + 1].wait()
        value = pair_product((held[2 * part], held[2 * part + 1]), right)
        chips = value.shape[0] // (2 * rows)
        for n in range(chips):
            slot = lax.rem(part * chips + n - chip + SIZES["z"], SIZES["z"])
            even = value[2 * n * rows : (2 * n + 1) * rows, :]
            odd = value[(2 * n + 1) * rows : (2 * n + 2) * rows, :]
            keep[slot] = jnp.where(core == 0, even, odd)
            give[slot] = jnp.where(core == 0, odd, even)


def second_image(place, turned, columns):
    depth, size = 2 * turned[0].shape[0], columns.shape[1]
    out = array(SIZES["z"], depth // (2 * SIZES["z"]), size)
    return call(
        second_image_kernel, (out, out), 3 * 10**9, limit=32 * 2**20,
        in_specs=[SMEM] + [APART] * len(turned) + [VMEM],
        out_specs=(VMEM, VMEM),
        scratch=[
            pltpu.VMEM((len(turned),) + turned[0].shape, BF16),
            pltpu.SemaphoreType.DMA((len(turned),)),
        ],
    )(place, *far_core(*turned), *near_core(columns))


def terms_kernel(place, second_sum, pieces, adjoint, factor, keep, give, rows, second_second, second_first, first_first):
    size = second_sum.shape[1]
    per = size // TILE
    middle = size // 2
    first_sum = pieces[0]
    for n in range(1, pieces.shape[0]):
        first_sum = first_sum + pieces[n]
    second = adjoint[1] - 2.0 * second_sum[...]
    first = adjoint[0] - 2.0 * first_sum
    rows[1], rows[0] = second, first

    def put(ref, at, cols, left, right):
        ref[at, cols] = pair_product(tuple(v[at, :] for v in left), tuple(v[:, cols] for v in right))

    second, first = split(second.T), split(first.T)
    second_right, first_right = split(factor[1]), split(factor[0])
    top, low, full = slice(0, middle), slice(middle, size), slice(0, size)
    put(second_first, full, full, second, first_right)
    put(second_second, top, top, second, second_right)
    put(second_second, low, full, second, second_right)
    put(first_first, top, top, first, first_right)
    put(first_first, low, full, first, first_right)

    lower = [(i, j) for i in range(per) for j in range(i + 1)]
    square = [(i, j) for i in range(per) for j in range(per)]
    tiles = [(second_second, at) for at in lower] + [(second_first, at) for at in square]
    tiles += [(first_first, at) for at in lower]
    half = len(tiles) // 2

    def store(out, chosen):
        for n, (ref, (i, j)) in enumerate(chosen):
            out[n * TILE : (n + 1) * TILE, :] = ref[
                i * TILE : (i + 1) * TILE, j * TILE : (j + 1) * TILE
            ]

    @pl.when(place[1] == 0)
    def _():
        store(keep, tiles[:half])
        store(give, tiles[half:])

    @pl.when(place[1] == 1)
    def _():
        store(keep, tiles[half:])
        store(give, tiles[:half])


def terms(place, second_sum, pieces, adjoint_low, factor_low):
    size = second_sum.shape[1]
    per = size // TILE
    half = per * (2 * per + 1) // 2 * TILE
    return call(
        terms_kernel, (array(half, TILE), array(half, TILE), array(*adjoint_low.shape)), 10**9, limit=32 * 2**20,
        in_specs=[SMEM] + [VMEM] * 4,
        out_specs=(VMEM,) * 3,
        scratch=[pltpu.VMEM((size, size), F32)] * 3,
    )(place, *near_core(second_sum, pieces), *far_core(adjoint_low, factor_low))


def rows_kernel(rows, inverses, solved, out):
    out[1] = 0.5 * matmul(rows[1], inverses[1])
    out[0] = 0.5 * matmul(rows[0] - matmul(rows[1], solved[...]), inverses[0])


def finish_kernel(
    place, mine, other, inverses_from, solved_from, second_from, first_from, adjoint_from, diag_to, top_to,
    second, cross, first, inverses, solved, second_const, first_const, adjoint_mid, diag, top, done,
):
    pairs = (
        (second_from, second_const),
        (solved_from, solved),
        (inverses_from, inverses),
        (first_from, first_const),
        (adjoint_from, adjoint_mid),
        (diag.at[0], diag_to.at[0]),
        (diag.at[1], diag_to.at[1]),
        (top, top_to),
    )
    copies = [pltpu.make_async_copy(x, y, done.at[n]) for n, (x, y) in enumerate(pairs)]
    for copy in copies[:5]:
        copy.start()
    size = solved.shape[0]
    core = place[1]
    per = size // TILE
    half = mine.shape[0] // TILE
    upper = lax.broadcasted_iota(jnp.int32, (TILE, TILE), 0) < lax.broadcasted_iota(
        jnp.int32, (TILE, TILE), 1
    )

    def tile(index):
        part, row = divmod(index, half)
        rows = slice(row * TILE, (row + 1) * TILE)
        return jnp.where(core == part, mine[rows, :], other[rows, :])

    def at(i, j):
        return (slice(i * TILE, (i + 1) * TILE), slice(j * TILE, (j + 1) * TILE))

    def mirror(value, ref):
        for i in range(per):
            for j in range(i + 1):
                part = value(i, j)
                if i == j:
                    ref[at(i, j)] = jnp.where(upper, part.T, part)
                else:
                    ref[at(i, j)] = part
                    ref[at(j, i)] = part.T

    low = per * (per + 1) // 2
    number = lambda i, j: i * (i + 1) // 2 + j
    for i in range(per):
        for j in range(per):
            cross[at(i, j)] = tile(low + i * per + j)
    copies[0].wait()
    mirror(lambda i, j: second_const[at(i, j)] - tile(number(i, j)), second)
    middle = size // 2
    whole, top_half, low_half = slice(0, size), slice(0, middle), slice(middle, size)

    def part(pair, rows, cols):
        return tuple(v[rows, cols] for v in pair)

    def times_lower(left, lower):
        return jnp.concatenate(
            [
                pair_product(left, part(lower, whole, top_half)),
                pair_product(part(left, whole, low_half), part(lower, low_half, low_half)),
            ],
            axis=1,
        )

    def upper_times(upper, right):
        return jnp.concatenate(
            [
                pair_product(part(upper, top_half, whole), right),
                pair_product(part(upper, low_half, low_half), part(right, low_half, whole)),
            ]
        )

    def between(upper, symmetric, lower, out):
        half_way = split(times_lower(symmetric, lower))
        out[top_half, top_half] = 0.5 * pair_product(
            part(upper, top_half, whole), part(half_way, whole, top_half)
        )
        bottom = 0.5 * pair_product(
            part(upper, low_half, low_half), part(half_way, low_half, whole)
        )
        out[low_half, whole] = bottom
        out[top_half, low_half] = bottom[:, top_half].T

    second_symmetric = split(second[...])
    copies[1].wait()
    image = pair_product(second_symmetric, split(solved[...]))
    outer = pair_product(split(solved[...].T), split(0.5 * image + cross[...]))
    outer = outer + outer.T

    def first_value(i, j):
        return first_const[at(i, j)] - tile(low + per * per + number(i, j)) + outer[at(i, j)]

    copies[3].wait()
    mirror(first_value, first)
    copies[2].wait()
    first_lower, second_lower = split(inverses[0]), split(inverses[1])
    first_upper, second_upper = split(inverses[0].T), split(inverses[1].T)
    between(first_upper, split(first[...]), first_lower, diag.at[0])
    copies[5].start()
    between(second_upper, second_symmetric, second_lower, diag.at[1])
    copies[6].start()
    copies[4].wait()
    rest = adjoint_mid[...] - upper_times(second_upper, split(image + cross[...]))
    top[...] = 0.5 * times_lower(split(rest), first_lower)
    copies[7].start()
    for copy in copies[5:]:
        copy.wait()


def finish(place, tiles, other, inverses, mid_solved, second_const, first_const, adjoint_mid):
    size = mid_solved.shape[0]
    return call(
        finish_kernel, (array(2, size, size), array(size, size)), 10**10, limit=32 * 2**20,
        in_specs=[SMEM] + [VMEM] * 2 + [APART] * 5, out_specs=(APART, APART),
        scratch=[pltpu.VMEM((size, size), F32)] * 3
        + [pltpu.VMEM((2, size, size), F32)]
        + [pltpu.VMEM((size, size), F32)] * 4
        + [pltpu.VMEM((2, size, size), F32), pltpu.VMEM((size, size), F32), pltpu.SemaphoreType.DMA((8,))],
    )(
        place, *near_core(tiles, other),
        *far_core(inverses, mid_solved, second_const, first_const, adjoint_mid),
    )


def shift(value, axis, step):
    size = SIZES[axis]
    return lax.ppermute(value, axis, [(i, (i + step) % size) for i in range(size)])


def ring_sum(blocks, axis):
    size = SIZES[axis]
    far = blocks[size // 2]
    half = far.shape[0] // 2
    ahead = shift(far[:half], axis, 1)
    behind = shift(far[half:], axis, -1)
    for step in range(size // 2 - 1, 0, -1):
        up, down = blocks[step], blocks[size - step]
        if step == size // 2 - 1:
            up = jnp.concatenate([up[:half] + ahead, up[half:]])
            down = jnp.concatenate([down[:half], down[half:] + behind])
        else:
            up, down = up + ahead, down + behind
        ahead, behind = shift(up, axis, 1), shift(down, axis, -1)
    return blocks[0] + ahead + behind


def column_sum(value):
    def flip(value, bits):
        return lax.ppermute(value, "z", [(i, i ^ bits) for i in range(SIZES["z"])])

    value = value + flip(value, 1)
    across = flip(value, 4)
    return (value + flip(value, 2)) + (across + flip(value, 6))


def spread(value, axes, parts):
    return lax.all_to_all(jnp.broadcast_to(value[None], (parts,) + value.shape), axes, 0, 0)


def shards(
    factor_diag, factor_mid, factor_low, adjoint_diag, adjoint_mid, adjoint_low, trailing_adjoint
):
    size = factor_mid.shape[0]
    rows = factor_low.shape[1]
    block_rows, row_groups, group_cols = trailing_adjoint.shape
    flipped = trailing_adjoint.transpose(1, 2, 0).reshape(row_groups * group_cols, block_rows)
    place = jnp.stack([lax.axis_index("z"), lax.axis_index("c")]).astype(jnp.int32)
    parts = SIZES["y"] * SIZES["x"]

    columns = spread(factor_low[1], ("y", "x"), parts).reshape(-1, size)

    own, half = factor_low[0], rows // 2
    ahead, behind = [own], [own]
    for _ in range(1, 4):
        ahead.append(shift(ahead[-1], "z", 1))
        behind.append(shift(behind[-1], "z", -1))
    across = jnp.concatenate([shift(ahead[3][:half], "z", 1), shift(behind[3][half:], "z", -1)])
    near = jnp.stack([own, ahead[1], behind[1], ahead[2], behind[2]])
    far = jnp.stack([ahead[3], behind[3], across])
    near_other, far_other = shift(near, "c", 1), shift(far, "c", 1)
    turned = turn(flipped, 0)
    turned += turn(flipped, 1)
    images = first_image(
        place, flipped, near, near_other, far, far_other
    )
    pieces = lax.all_to_all(images.reshape(parts, rows, size), ("y", "x"), 0, 0)
    keep, give = second_image(place, turned, columns)
    give = shift(give, "c", 1)
    second_sum = ring_sum(keep + give, "z")

    keep, give, sides = terms(place, second_sum, pieces, adjoint_low, factor_low)
    keep = keep + shift(give, "c", 1)
    tiles = lax.all_to_all(keep.reshape(parts, -1, TILE), ("y", "x"), 0, 0)
    tiles = column_sum(tiles.sum(0))
    tiles = spread(tiles, ("y", "x"), parts).reshape(-1, TILE)
    other = shift(tiles, "c", 1)
    inverses = invert(factor_diag)
    mid_solved, second_const, first_const = constants(
        factor_diag, factor_mid, adjoint_diag, adjoint_mid, inverses
    )
    low = call(
        rows_kernel, array(2, rows, size), 10**9, in_specs=[VMEM] * 3, out_specs=VMEM
    )(*far_core(sides, inverses, mid_solved))
    diag, top = finish(place, tiles, other, inverses, mid_solved, second_const, first_const, adjoint_mid)
    return diag, top, low


def solution(mesh):
    axes = tuple(SIZES)
    torus = Mesh(mesh.devices.reshape(tuple(SIZES.values())), axes)
    low = P(None, axes, None)

    return jax.shard_map(
        shards,
        mesh=torus,
        in_specs=(P(), P(), low, P(), P(), low, P(("y", "x"), None, ("z", "c"))),
        out_specs=(P(), P(), low),
        check_vma=False,
    )
```

```python
import functools
import jax
import jax.numpy as jnp
from jax import lax
from jax.experimental import pallas as pl
from jax.experimental.pallas import tpu as pltpu
from jax.sharding import Mesh, PartitionSpec as P

SIZES = {"y": 4, "x": 4, "z": 8, "c": 2}
TILE = 128


F32 = jnp.float32
BF16 = jnp.bfloat16
VMEM = pl.BlockSpec(memory_space=pltpu.VMEM)
SMEM = pl.BlockSpec(memory_space=pltpu.SMEM)
APART = pl.BlockSpec(memory_space=pl.ANY)
NN, TN = ((1,), (0,)), ((0,), (0,))


def product(left_side, right_side, dims=NN):
    return lax.dot_general(
        left_side, right_side, (dims, ((), ())), precision=lax.Precision.HIGHEST, preferred_element_type=F32
    )


def split(value):
    high = value.astype(BF16)
    return high, (value - high.astype(F32)).astype(BF16)


def pair_product(left_side, right_side, dims=NN):
    one = functools.partial(lax.dot_general, dimension_numbers=(dims, ((), ())), preferred_element_type=F32)
    return (
        one(left_side[0], right_side[0])
        + (one(left_side[0], right_side[1]) + one(left_side[1], right_side[0]))
    )


def call(kernel, outs, flops, grid=None, in_specs=None, out_specs=None, scratch=(), limit=None):
    specs = {} if grid is None else {"grid": grid}
    return pl.pallas_call(
        kernel,
        out_shape=outs,
        in_specs=in_specs,
        out_specs=out_specs,
        scratch_shapes=scratch,
        compiler_params=pltpu.CompilerParams(vmem_limit_bytes=limit),
        cost_estimate=pl.CostEstimate(flops=flops, bytes_accessed=8 * 2**20, transcendentals=0),
        **specs,
    )


def array(*shape):
    return jax.ShapeDtypeStruct(shape, F32)


def near_core(*values):
    return tuple(pltpu.with_memory_space_constraint(v, pltpu.VMEM) for v in values)


def far_core(*values):
    return tuple(pltpu.with_memory_space_constraint(v, pltpu.HBM) for v in values)


def matmul(left_side, right_side, dims=NN):
    if dims == TN:
        left_side = left_side.T
    return pair_product(split(left_side), split(right_side))


def invert_kernel(factor, out, blocks, parts):
    count, size = factor.shape[0], factor.shape[1]
    row = lax.broadcasted_iota(jnp.int32, (TILE, TILE), 0)
    column = lax.broadcasted_iota(jnp.int32, (TILE, TILE), 1)
    eye = row == column
    per = size // TILE
    for p in range(count):
        for b in range(per):
            at = slice(b * TILE, (b + 1) * TILE)
            block = factor[p, at, at]
            blocks[p * per + b] = block
            parts[p * per + b] = jnp.where(eye, 1.0 / jnp.where(eye, block, 1.0), 0.0)

    def level(index, carry):
        step, group = lax.div(index, count), lax.rem(index, count) * per
        high, low = lax.shift_right_logical(row, step), lax.shift_right_logical(column, step)
        corner = (high == low + 1) & ((high & 1) == 1)
        slots = [group + b for b in range(per)]
        halves = [product(jnp.where(corner, blocks[s], 0.0), parts[s]) for s in slots]
        news = [parts[s] - product(parts[s], half) for s, half in zip(slots, halves)]
        for s, new in zip(slots, news):
            parts[s] = new
        return carry

    lax.fori_loop(0, (TILE.bit_length() - 1) * count, level, 0)
    out[...] = jnp.zeros_like(out)
    for p in range(count):
        for b in range(per):
            at = slice(b * TILE, (b + 1) * TILE)
            out[p, at, at] = parts[p * per + b]

    def joined(p, carry):
        step = TILE
        while step < size:
            for start in range(0, size, 2 * step):
                low, mid, high = start, start + step, start + 2 * step
                half = product(factor[p, mid:high, low:mid], out[p, low:mid, low:mid])
                out[p, mid:high, low:mid] = -product(out[p, mid:high, mid:high], half)
            step *= 2
        return carry

    lax.fori_loop(0, count, joined, 0)


def invert(factor_diag):
    count, size = factor_diag.shape[0], factor_diag.shape[1]
    blocks = pltpu.VMEM((count * size // TILE, TILE, TILE), F32)
    return call(
        invert_kernel, array(*factor_diag.shape), 10**10,
        in_specs=[VMEM], out_specs=VMEM, scratch=[blocks, blocks],
    )(*far_core(factor_diag))


def constants_kernel(factor, mid, adjoint, adjoint_mid, inverses, solved, second, first):
    solved[...] = matmul(inverses[1], mid[...])

    def inner(panel, carry):
        value = matmul(factor[panel], adjoint[panel], TN)

        @pl.when(panel == 0)
        def _():
            first[...] = value

        @pl.when(panel == 1)
        def _():
            second[...] = value

        return carry

    lax.fori_loop(0, 2, inner, 0)
    first[...] = first[...] - matmul(adjoint_mid[...], mid[...], TN)


def constants(factor_diag, factor_mid, adjoint_diag, adjoint_mid, inverses):
    square = array(*factor_mid.shape)
    return call(
        constants_kernel, (square, square, square), 5 * 10**9,
        in_specs=[VMEM] * 5, out_specs=(VMEM,) * 3,
    )(*far_core(factor_diag, factor_mid, adjoint_diag, adjoint_mid, inverses))


def turn_kernel(block, high, low):
    high[...], low[...] = split(block[...].T)


def turn(flipped, part):
    count, depth = flipped.shape
    step = min(256, depth // 2)
    steps = depth // 2 // step
    out = jax.ShapeDtypeStruct((depth // 2, count), BF16)
    tall = pl.BlockSpec((step, count), lambda i: (i, 0))
    return call(
        turn_kernel, (out, out), 10**9,
        grid=(steps,),
        in_specs=[pl.BlockSpec((count, step), lambda i: (0, part * steps + i))],
        out_specs=(tall, tall),
    )(*far_core(flipped))


def first_image_kernel(place, block, near, near_other, far, far_other, out, high, low):
    chip, core = place[0], place[1]
    rows = near.shape[1]

    @pl.when(pl.program_id(0) == 0)
    def _():
        start = 0
        for mine, other in ((near, near_other), (far, far_other)):

            def put(slot, carry, start=start, mine=mine, other=other):
                index = start + slot
                distance = lax.div(index + 1, 2)
                offset = jnp.where(lax.rem(index, 2) == 1, -distance, distance)
                at = lax.rem(chip + offset + SIZES["z"], SIZES["z"]) * 2
                for ref, owner in ((mine, core), (other, 1 - core)):
                    where = pl.ds(pl.multiple_of((at + owner) * rows, rows), rows)
                    high[where, :], low[where, :] = split(ref[slot])
                return carry

            lax.fori_loop(0, mine.shape[0], put, 0)
            start += mine.shape[0]

    out[...] = pair_product(split(block[...]), (high[...], low[...]))


def first_image(place, flipped, near, near_other, far, far_other):
    count, depth = flipped.shape
    size = near.shape[2]
    step = min(512, count)
    gathered = near_core(near, near_other, far, far_other)
    return call(
        first_image_kernel, array(count, size), 3 * 10**9, limit=32 * 2**20,
        grid=(count // step,),
        in_specs=[SMEM, pl.BlockSpec((step, depth), lambda i: (i, 0))] + [VMEM] * 4,
        out_specs=pl.BlockSpec((step, size), lambda i: (i, 0)),
        scratch=[pltpu.VMEM((depth, size), BF16)] * 2,
    )(place, *far_core(flipped), *gathered)


def second_image_kernel(place, *refs):
    turned, (columns, keep, give, held, done) = refs[:-5], refs[-5:]
    chip, core = place[0], place[1]
    rows = keep.shape[1]
    copies = [pltpu.make_async_copy(v, held.at[n], done.at[n]) for n, v in enumerate(turned)]
    for copy in copies:
        copy.start()
    right = split(columns[...])
    for copy in copies:
        copy.wait()

    def half(part, carry):
        value = pair_product((held[2 * part], held[2 * part + 1]), right)
        chips = value.shape[0] // (2 * rows)
        for n in range(chips):
            slot = lax.rem(part * chips + n - chip + SIZES["z"], SIZES["z"])
            even = value[2 * n * rows : (2 * n + 1) * rows, :]
            odd = value[(2 * n + 1) * rows : (2 * n + 2) * rows, :]
            keep[slot] = jnp.where(core == 0, even, odd)
            give[slot] = jnp.where(core == 0, odd, even)
        return carry

    lax.fori_loop(0, len(turned) // 2, half, 0)


def second_image(place, turned, columns):
    depth, size = 2 * turned[0].shape[0], columns.shape[1]
    out = array(SIZES["z"], depth // (2 * SIZES["z"]), size)
    return call(
        second_image_kernel, (out, out), 3 * 10**9, limit=32 * 2**20,
        in_specs=[SMEM] + [APART] * len(turned) + [VMEM],
        out_specs=(VMEM, VMEM),
        scratch=[
            pltpu.VMEM((len(turned),) + turned[0].shape, BF16),
            pltpu.SemaphoreType.DMA((len(turned),)),
        ],
    )(place, *far_core(*turned), *near_core(columns))


def terms_kernel(place, second_sum, pieces, adjoint, factor, keep, give, rows, second_second, second_first, first_first):
    size = second_sum.shape[1]
    per = size // TILE
    middle = size // 2
    first_sum = pieces[0]
    for n in range(1, pieces.shape[0]):
        first_sum = first_sum + pieces[n]
    second = adjoint[1] - 2.0 * second_sum[...]
    first = adjoint[0] - 2.0 * first_sum
    rows[1], rows[0] = second, first

    def put(ref, at, cols, left, right):
        ref[at, cols] = pair_product(tuple(v[at, :] for v in left), tuple(v[:, cols] for v in right))

    second, first = split(second.T), split(first.T)
    second_right, first_right = split(factor[1]), split(factor[0])
    top, low, full = slice(0, middle), slice(middle, size), slice(0, size)
    put(second_first, full, full, second, first_right)
    put(second_second, top, top, second, second_right)
    put(second_second, low, full, second, second_right)
    put(first_first, top, top, first, first_right)
    put(first_first, low, full, first, first_right)

    lower = [(i, j) for i in range(per) for j in range(i + 1)]
    square = [(i, j) for i in range(per) for j in range(per)]
    tiles = [(second_second, at) for at in lower] + [(second_first, at) for at in square]
    tiles += [(first_first, at) for at in lower]
    half = len(tiles) // 2

    def store(out, chosen):
        for n, (ref, (i, j)) in enumerate(chosen):
            out[n * TILE : (n + 1) * TILE, :] = ref[
                i * TILE : (i + 1) * TILE, j * TILE : (j + 1) * TILE
            ]

    @pl.when(place[1] == 0)
    def _():
        store(keep, tiles[:half])
        store(give, tiles[half:])

    @pl.when(place[1] == 1)
    def _():
        store(keep, tiles[half:])
        store(give, tiles[:half])


def terms(place, second_sum, pieces, adjoint_low, factor_low):
    size = second_sum.shape[1]
    per = size // TILE
    half = per * (2 * per + 1) // 2 * TILE
    return call(
        terms_kernel, (array(half, TILE), array(half, TILE), array(*adjoint_low.shape)), 10**9, limit=32 * 2**20,
        in_specs=[SMEM] + [VMEM] * 4,
        out_specs=(VMEM,) * 3,
        scratch=[pltpu.VMEM((size, size), F32)] * 3,
    )(place, *near_core(second_sum, pieces), *far_core(adjoint_low, factor_low))


def rows_kernel(rows, inverses, solved, out):
    out[1] = 0.5 * matmul(rows[1], inverses[1])
    out[0] = 0.5 * matmul(rows[0] - matmul(rows[1], solved[...]), inverses[0])


def finish_kernel(
    place, mine, other, inverses_from, solved_from, second_from, first_from, adjoint_from, diag_to, top_to,
    second, cross, first, inverses, solved, second_const, first_const, adjoint_mid, diag, top, done,
):
    pairs = (
        (second_from, second_const),
        (solved_from, solved),
        (inverses_from, inverses),
        (first_from, first_const),
        (adjoint_from, adjoint_mid),
        (diag.at[0], diag_to.at[0]),
        (diag.at[1], diag_to.at[1]),
        (top, top_to),
    )
    copies = [pltpu.make_async_copy(x, y, done.at[n]) for n, (x, y) in enumerate(pairs)]
    for copy in copies[:5]:
        copy.start()
    size = solved.shape[0]
    core = place[1]
    per = size // TILE
    half = mine.shape[0] // TILE
    upper = lax.broadcasted_iota(jnp.int32, (TILE, TILE), 0) < lax.broadcasted_iota(
        jnp.int32, (TILE, TILE), 1
    )

    def tile(index):
        part, row = divmod(index, half)
        rows = slice(row * TILE, (row + 1) * TILE)
        return jnp.where(core == part, mine[rows, :], other[rows, :])

    def at(i, j):
        return (slice(i * TILE, (i + 1) * TILE), slice(j * TILE, (j + 1) * TILE))

    def mirror(value, ref):
        for i in range(per):
            for j in range(i + 1):
                part = value(i, j)
                if i == j:
                    ref[at(i, j)] = jnp.where(upper, part.T, part)
                else:
                    ref[at(i, j)] = part
                    ref[at(j, i)] = part.T

    low = per * (per + 1) // 2
    number = lambda i, j: i * (i + 1) // 2 + j
    for i in range(per):
        for j in range(per):
            cross[at(i, j)] = tile(low + i * per + j)
    copies[0].wait()
    mirror(lambda i, j: second_const[at(i, j)] - tile(number(i, j)), second)
    middle = size // 2
    whole, top_half, low_half = slice(0, size), slice(0, middle), slice(middle, size)

    def part(pair, rows, cols):
        return tuple(v[rows, cols] for v in pair)

    def times_lower(left, lower):
        return jnp.concatenate(
            [
                pair_product(left, part(lower, whole, top_half)),
                pair_product(part(left, whole, low_half), part(lower, low_half, low_half)),
            ],
            axis=1,
        )

    def upper_times(upper, right):
        return jnp.concatenate(
            [
                pair_product(part(upper, top_half, whole), right),
                pair_product(part(upper, low_half, low_half), part(right, low_half, whole)),
            ]
        )

    def between(upper, symmetric, lower, out):
        half_way = split(times_lower(symmetric, lower))
        out[top_half, top_half] = 0.5 * pair_product(
            part(upper, top_half, whole), part(half_way, whole, top_half)
        )
        bottom = 0.5 * pair_product(
            part(upper, low_half, low_half), part(half_way, low_half, whole)
        )
        out[low_half, whole] = bottom
        out[top_half, low_half] = bottom[:, top_half].T

    second_symmetric = split(second[...])
    copies[1].wait()
    image = pair_product(second_symmetric, split(solved[...]))
    outer = pair_product(split(solved[...].T), split(0.5 * image + cross[...]))
    outer = outer + outer.T

    def first_value(i, j):
        return first_const[at(i, j)] - tile(low + per * per + number(i, j)) + outer[at(i, j)]

    copies[3].wait()
    mirror(first_value, first)
    copies[2].wait()
    first_lower, second_lower = split(inverses[0]), split(inverses[1])
    first_upper, second_upper = split(inverses[0].T), split(inverses[1].T)
    between(first_upper, split(first[...]), first_lower, diag.at[0])
    copies[5].start()
    between(second_upper, second_symmetric, second_lower, diag.at[1])
    copies[6].start()
    copies[4].wait()
    rest = adjoint_mid[...] - upper_times(second_upper, split(image + cross[...]))
    top[...] = 0.5 * times_lower(split(rest), first_lower)
    copies[7].start()
    for copy in copies[5:]:
        copy.wait()


def finish(place, tiles, other, inverses, mid_solved, second_const, first_const, adjoint_mid):
    size = mid_solved.shape[0]
    return call(
        finish_kernel, (array(2, size, size), array(size, size)), 10**10, limit=32 * 2**20,
        in_specs=[SMEM] + [VMEM] * 2 + [APART] * 5, out_specs=(APART, APART),
        scratch=[pltpu.VMEM((size, size), F32)] * 3
        + [pltpu.VMEM((2, size, size), F32)]
        + [pltpu.VMEM((size, size), F32)] * 4
        + [pltpu.VMEM((2, size, size), F32), pltpu.VMEM((size, size), F32), pltpu.SemaphoreType.DMA((8,))],
    )(
        place, *near_core(tiles, other),
        *far_core(inverses, mid_solved, second_const, first_const, adjoint_mid),
    )


def shift(value, axis, step):
    size = SIZES[axis]
    return lax.ppermute(value, axis, [(i, (i + step) % size) for i in range(size)])


def ring_sum(blocks, axis):
    size = SIZES[axis]
    far = blocks[size // 2]
    half = far.shape[0] // 2
    ahead = shift(far[:half], axis, 1)
    behind = shift(far[half:], axis, -1)
    for step in range(size // 2 - 1, 0, -1):
        up, down = blocks[step], blocks[size - step]
        if step == size // 2 - 1:
            up = jnp.concatenate([up[:half] + ahead, up[half:]])
            down = jnp.concatenate([down[:half], down[half:] + behind])
        else:
            up, down = up + ahead, down + behind
        ahead, behind = shift(up, axis, 1), shift(down, axis, -1)
    return blocks[0] + ahead + behind


def column_sum(value):
    def flip(value, bits):
        return lax.ppermute(value, "z", [(i, i ^ bits) for i in range(SIZES["z"])])

    value = value + flip(value, 1)
    across = flip(value, 4)
    return (value + flip(value, 2)) + (across + flip(value, 6))


def spread(value, axes, parts):
    return lax.all_to_all(jnp.broadcast_to(value[None], (parts,) + value.shape), axes, 0, 0)


def shards(
    factor_diag, factor_mid, factor_low, adjoint_diag, adjoint_mid, adjoint_low, trailing_adjoint
):
    size = factor_mid.shape[0]
    rows = factor_low.shape[1]
    block_rows, row_groups, group_cols = trailing_adjoint.shape
    flipped = trailing_adjoint.transpose(1, 2, 0).reshape(row_groups * group_cols, block_rows)
    place = jnp.stack([lax.axis_index("z"), lax.axis_index("c")]).astype(jnp.int32)
    parts = SIZES["y"] * SIZES["x"]

    columns = spread(factor_low[1], ("y", "x"), parts).reshape(-1, size)

    own, half = factor_low[0], rows // 2
    ahead, behind = [own], [own]
    for _ in range(1, 4):
        ahead.append(shift(ahead[-1], "z", 1))
        behind.append(shift(behind[-1], "z", -1))
    across = jnp.concatenate([shift(ahead[3][:half], "z", 1), shift(behind[3][half:], "z", -1)])
    near = jnp.stack([own, ahead[1], behind[1], ahead[2], behind[2]])
    far = jnp.stack([ahead[3], behind[3], across])
    near_other, far_other = shift(near, "c", 1), shift(far, "c", 1)
    turned = turn(flipped, 0)
    turned += turn(flipped, 1)
    images = first_image(
        place, flipped, near, near_other, far, far_other
    )
    pieces = lax.all_to_all(images.reshape(parts, rows, size), ("y", "x"), 0, 0)
    keep, give = second_image(place, turned, columns)
    give = shift(give, "c", 1)
    second_sum = ring_sum(keep + give, "z")

    keep, give, sides = terms(place, second_sum, pieces, adjoint_low, factor_low)
    keep = keep + shift(give, "c", 1)
    tiles = lax.all_to_all(keep.reshape(parts, -1, TILE), ("y", "x"), 0, 0)
    tiles = column_sum(tiles.sum(0))
    tiles = spread(tiles, ("y", "x"), parts).reshape(-1, TILE)
    other = shift(tiles, "c", 1)
    inverses = invert(factor_diag)
    mid_solved, second_const, first_const = constants(
        factor_diag, factor_mid, adjoint_diag, adjoint_mid, inverses
    )
    low = call(
        rows_kernel, array(2, rows, size), 10**9, in_specs=[VMEM] * 3, out_specs=VMEM
    )(*far_core(sides, inverses, mid_solved))
    diag, top = finish(place, tiles, other, inverses, mid_solved, second_const, first_const, adjoint_mid)
    return diag, top, low


def solution(mesh):
    axes = tuple(SIZES)
    torus = Mesh(mesh.devices.reshape(tuple(SIZES.values())), axes)
    low = P(None, axes, None)

    return jax.shard_map(
        shards,
        mesh=torus,
        in_specs=(P(), P(), low, P(), P(), low, P(("y", "x"), None, ("z", "c"))),
        out_specs=(P(), P(), low),
        check_vma=False,
    )
```
